32 devices in a mesh: slab: 8 (over z, y), patch: 4 (over x, core).
Axes of the slice: x: 2, y: 2, z: 4, core: 2. Of those that a mesh axis runs over, the one named last changes fastest.
Arguments:
- fluid_state: float32 [16, 256, 256], P('slab', 'patch'), may hold values from -6 to 6
- fluid_rhs: float32 [16, 256, 256], P('slab', 'patch'), may hold values from -24 to 24
- element_scale: float32 [16, 256], P('slab', 'patch'), may hold values from 1 to 4
- element_matrix: bfloat16 [256, 256], replicated
- couple_x: bfloat16 [256, 256], replicated, may hold values from -0.09375 to 0.09375
- couple_y: bfloat16 [256, 256], replicated, may hold values from -0.09375 to 0.09375
- block_inverse: bfloat16 [256, 256], replicated
- traction_map: bfloat16 [3, 256], replicated, may hold values from -0.375 to 0.375
- slot_elem: int32 [8, 4, 1024], P('slab', 'patch'), may hold values from 0 to 127
- slot_point: int32 [8, 4, 1024], P('slab', 'patch'), may hold values from 0 to 8191
- slot_count: int32 [8, 4, 4], P('slab', 'patch'), may hold values from 0 to 256, as said below
- displacement: float32 [3, 256, 128], P(None, 'patch'), may hold values from -6 to 6
- stiffness: float32 [256, 128], P('patch'), may hold values from 0.03 to 0.3
Outputs:
- fluid_out: float32 [16, 256, 256], P('slab', 'patch')
- displacement_new: float32 [3, 256, 128], P(None, 'patch')
- wall_motion: float32 [3, 8, 4, 1024], P(None, 'slab', 'patch')
The draws below stay inside these ranges and needn't reach their ends.
Inputs may be any that keep to these rules, and one draw needn't show every extreme that they name: For every block and owner only the first slot_count slots of that owner's 256 slots are live; the count 256 is reached for some block and owner in every draw.
All inputs are finite; a program needn't handle non-finite values.
Results may differ from the reference program's by a relative error of at most 0.0049.
Values may be sent and summed in bfloat16 or wider, within the bound.
A program may use at most 128 MiB of HBM per device.

```python
import math
import jax
import jax.numpy as jnp

DOF = 256
EX_DEV = 2
EY_DEV = 64
SWEEPS = 3
NU = 64
NV = 128
CAP = 256
QDEV = 1024
NX = 16
NY = 256
NU_ALL = 256
N_SLAB = 8
N_PATCH = 4


def draw_element_matrix(key, part):
    noise = jax.random.normal(jax.random.fold_in(key, 3), (DOF, DOF), jnp.float32)
    return (4.0 * jnp.eye(DOF, dtype=jnp.float32) + noise / jnp.sqrt(DOF * 1.0)).astype(jnp.bfloat16)


def draw_block_inverse(key, part):
    noise = jax.random.normal(jax.random.fold_in(key, 5), (DOF, DOF), jnp.float32)
    return (0.25 * jnp.eye(DOF, dtype=jnp.float32) + 0.1 * noise / jnp.sqrt(DOF * 1.0)).astype(jnp.bfloat16)


def draw_slot_count(key, part):
    first, second = jax.random.split(jax.random.fold_in(key, 11), 2)
    base = jax.random.randint(first, (N_SLAB, N_PATCH, N_PATCH), CAP // 2, CAP + 1)
    slab_rank = jnp.arange(N_SLAB, dtype=jnp.int32)[:, None, None]
    counts = (base * (slab_rank + 1) // N_SLAB).reshape(-1)
    chosen = jax.random.randint(second, (), 0, N_SLAB * N_PATCH * N_PATCH)
    counts = counts.at[chosen].set(CAP)
    return counts.reshape(N_SLAB, N_PATCH, N_PATCH).astype(jnp.int32)


def plant(values, stream_key, least, largest):
    extent = values.shape
    place = [jax.random.randint(jax.random.fold_in(stream_key, axis), (), 0, extent[axis]) for axis in range(len(extent))]
    values = values.at[tuple(place)].set(least)
    longest = extent.index(max(extent))
    place[longest] = (place[longest] + 1) % extent[longest]
    return values.at[tuple(place)].set(largest)


def steps_of(key, extent, pieces, low, largest):
    loudness = 1.0
    for position, shards_of in pieces:
        steps = jax.random.uniform(jax.random.fold_in(jax.random.fold_in(key, 6), position), (shards_of,), jnp.float32, low / len(pieces), largest / len(pieces))
        loudness = loudness * jnp.repeat(jnp.exp(steps), extent[position] // shards_of).reshape((-1,) + (1,) * (len(extent) - 1 - position))
    return loudness


def centred(rng, dims, scale, reach, cuts=(), kind=jnp.bfloat16):
    array = jax.random.normal(rng, dims, jnp.float32) * scale
    if len(cuts) > 0:
        array = steps_of(rng, dims, cuts, -0.22, 0.18) * array
    return jnp.clip(array, min=-reach, max=reach).astype(kind)


def setup_inputs(seed: int = 0) -> dict:
    streams_of = jax.random.split(jax.random.key(seed), 14)
    fluid_state = centred(streams_of[0], (NX, NY, DOF), 1.0, 6.0, ((0, 8), (1, 4)), jnp.float32)
    fluid_rhs = centred(streams_of[1], (NX, NY, DOF), 4.0, 24.0, ((0, 8), (1, 4)), jnp.float32)
    element_scale = jnp.clip(jnp.exp(math.log(4.0) - 1.3862944 * jax.random.uniform(streams_of[2], (NX, NY), jnp.float32) ** steps_of(streams_of[2], (NX, NY), ((0, 8), (1, 4)), -0.2, 0.2)), 1.0, 4.0)
    element_matrix = draw_element_matrix(jax.random.fold_in(streams_of[13], 71), 0)
    couple_x = centred(streams_of[4], (DOF, DOF), (16 * DOF) ** -0.5, 0.09375)
    couple_y = centred(streams_of[5], (DOF, DOF), (16 * DOF) ** -0.5, 0.09375)
    block_inverse = draw_block_inverse(jax.random.fold_in(streams_of[13], 71), 0)
    traction_map = centred(streams_of[7], (3, DOF), DOF ** -0.5, 0.375)
    slot_elem = plant(jax.random.randint(streams_of[8], (N_SLAB, N_PATCH, QDEV), 0, EX_DEV * EY_DEV), jax.random.fold_in(streams_of[8], 1), 0, (EX_DEV * EY_DEV) - 1).astype(jnp.int32)
    slot_point = plant(jax.random.randint(streams_of[9], (N_SLAB, N_PATCH, QDEV), 0, NU * NV), jax.random.fold_in(streams_of[9], 1), 0, (NU * NV) - 1).astype(jnp.int32)
    slot_count = draw_slot_count(jax.random.fold_in(streams_of[13], 71), 0)
    displacement = centred(streams_of[11], (3, NU_ALL, NV), 1.0, 6.0, ((1, 4),), jnp.float32)
    stiffness = jnp.clip(jnp.exp(math.log(0.3) - 2.3025852 * jax.random.uniform(streams_of[12], (NU_ALL, NV), jnp.float32) ** steps_of(streams_of[12], (NU_ALL, NV), ((0, 4),), -0.2, 0.2)), 0.03, 0.3)
    return {"fluid_state": fluid_state, "fluid_rhs": fluid_rhs, "element_scale": element_scale, "element_matrix": element_matrix, "couple_x": couple_x, "couple_y": couple_y, "block_inverse": block_inverse, "traction_map": traction_map, "slot_elem": slot_elem, "slot_point": slot_point, "slot_count": slot_count, "displacement": displacement, "stiffness": stiffness}


def element_apply(rounded, scale, element_matrix, couple_x, couple_y):
    padded = jnp.pad(rounded, ((1, 1), (1, 1), (0, 0)))
    along_x = (padded[:-2, 1:-1].astype(jnp.float32) + padded[2:, 1:-1].astype(jnp.float32)).astype(jnp.bfloat16)
    along_y = (padded[1:-1, :-2].astype(jnp.float32) + padded[1:-1, 2:].astype(jnp.float32)).astype(jnp.bfloat16)
    width = rounded.shape[2]
    own = jnp.dot(rounded.reshape(-1, width), element_matrix, preferred_element_type=jnp.float32)
    side_x = jnp.dot(along_x.reshape(-1, width), couple_x, preferred_element_type=jnp.float32)
    side_y = jnp.dot(along_y.reshape(-1, width), couple_y, preferred_element_type=jnp.float32)
    return scale[:, :, None] * own.reshape(rounded.shape) - side_x.reshape(rounded.shape) - side_y.reshape(rounded.shape)


def laplace_net(field):
    edged = jnp.pad(field, ((0, 0), (1, 1), (1, 1)))
    return 4.0 * field - (edged[:, 2:, 1:-1] + edged[:, :-2, 1:-1] + edged[:, 1:-1, 2:] + edged[:, 1:-1, :-2])


def pick_rows(block, picks):
    return block[picks]


def reference(fluid_state, fluid_rhs, element_scale, element_matrix, couple_x, couple_y, block_inverse, traction_map, slot_elem, slot_point, slot_count, displacement, stiffness):
    state = fluid_state
    for sweep in range(SWEEPS):
        rounded = state.astype(jnp.bfloat16)
        applied = element_apply(rounded, element_scale, element_matrix, couple_x, couple_y)
        residue = (fluid_rhs - applied).astype(jnp.bfloat16)
        update = jnp.dot(residue.reshape(-1, DOF), block_inverse, preferred_element_type=jnp.float32).reshape(state.shape)
        state = state + update / element_scale[:, :, None]
    fluid_out = state
    final = fluid_out.astype(jnp.bfloat16)
    blocks = final.reshape(N_SLAB, EX_DEV, N_PATCH, EY_DEV, DOF).transpose(0, 2, 1, 3, 4).reshape(N_SLAB, N_PATCH, EX_DEV * EY_DEV, DOF)
    rows = jax.vmap(jax.vmap(pick_rows))(blocks, slot_elem)
    pull = jnp.einsum("cd,snqd->csnq", traction_map.astype(jnp.float32), rows.astype(jnp.float32))
    slot_ids = jnp.arange(QDEV, dtype=jnp.int32)
    owner = slot_ids // CAP
    limit = jnp.take(slot_count, owner, axis=2)
    live = ((slot_ids % CAP)[None, None, :] < limit).astype(jnp.float32)
    target = owner[None, None, :] * (NU * NV) + slot_point
    loads = jnp.zeros((3, N_PATCH * NU * NV), jnp.float32).at[:, target.reshape(-1)].add((pull * live[None]).reshape(3, -1))
    loads = loads.reshape(3, NU_ALL, NV)
    bend = laplace_net(displacement)
    stiff_term = stiffness[None] * (laplace_net(bend) + 4.0 * bend)
    displacement_new = displacement + (loads - stiff_term) / (36.0 * stiffness[None])
    wall_motion = displacement_new.reshape(3, -1)[:, target.reshape(-1)].reshape(3, N_SLAB, N_PATCH, QDEV) * live[None]
    return fluid_out, displacement_new, wall_motion
```

```python
import functools

import jax
import jax.numpy as jnp
from jax import lax
from jax.experimental import pallas as pl
from jax.experimental.pallas import tpu as pltpu
from jax.sharding import PartitionSpec as P

SWEEPS = 3
PACK = 16
EDGE = 8
MESH = pl.DeviceIdType.MESH
F32 = jnp.float32
BF16 = jnp.bfloat16


def dot(a, b):
    return jnp.dot(a, b, preferred_element_type=F32)


def dot_nt(a, b):
    return lax.dot_general(a, b, (((1,), (1,)), ((), ())), preferred_element_type=F32)


def split_point(point, cols):
    if cols & (cols - 1) == 0:
        return lax.shift_right_logical(point, cols.bit_length() - 1), point & (cols - 1)
    row = lax.div(point, cols)
    return row, point - row * cols


def column(row_vector):
    n = row_vector.shape[1]
    shape = (n, n)
    eye = lax.broadcasted_iota(jnp.int32, shape, 0) == lax.broadcasted_iota(jnp.int32, shape, 1)
    return jnp.sum(jnp.where(eye, jnp.broadcast_to(row_vector, shape), 0.0), axis=1, keepdims=True)


def laplace(x):
    rows, cols = x.shape
    lane = lax.broadcasted_iota(jnp.int32, x.shape, 1)
    left = jnp.where(lane == 0, 0.0, pltpu.roll(x, 1, 1))
    right = jnp.where(lane == cols - 1, 0.0, pltpu.roll(x, cols - 1, 1))
    return 4.0 * x - (pltpu.roll(x, 1, 0) + pltpu.roll(x, rows - 1, 0) + left + right)


def kernel(
    slabs,
    patches,
    state_ref,
    rhs_ref,
    scale_ref,
    matrix_ref,
    cx_ref,
    cy_ref,
    inverse_ref,
    traction_ref,
    elem_ref,
    point_ref,
    count_ref,
    disp_ref,
    stiff_ref,
    fluid_ref,
    net_ref,
    wall_ref,
    vb,
    halo_x,
    halo_y,
    halo_d,
    points,
    pulls,
    pull_out,
    picks_out,
    picks_in,
    onehot_elem,
    onehot_row,
    onehot_col,
    kd_buf,
    sx,
    rx,
    sy,
    ry,
    sd,
    rd,
    sp1,
    rp1,
    sp2,
    rp2,
    sq1,
    rq1,
    sq2,
    rq2,
    sw,
    rw,
):
    s = lax.axis_index("slab")
    p = lax.axis_index("patch")
    ex, ey, dof = state_ref.shape
    comps, rows, cols = disp_ref.shape
    cap = elem_ref.shape[2] // patches

    def slab_peer(j):
        return lax.rem(s + j, slabs)

    def patch_peer(j):
        return lax.rem(p + j, patches)

    barrier = pltpu.get_barrier_semaphore()
    for j in range(1, slabs):
        pl.semaphore_signal(barrier, inc=1, device_id=(slab_peer(j), p), device_id_type=MESH)
    for j in range(1, patches):
        pl.semaphore_signal(barrier, inc=1, device_id=(s, patch_peer(j)), device_id_type=MESH)

    def remote(src, dst, send, recv, target):
        return pltpu.make_async_remote_copy(
            src_ref=src, dst_ref=dst, send_sem=send, recv_sem=recv, device_id=target, device_id_type=MESH
        )

    def x_up(k):
        return remote(vb.at[k, ex - 1], halo_x.at[k, 0], sx.at[k, 0], rx.at[k, 0], (jnp.minimum(s + 1, slabs - 1), p))

    def x_down(k):
        return remote(vb.at[k, 0], halo_x.at[k, 1], sx.at[k, 1], rx.at[k, 1], (jnp.maximum(s - 1, 0), p))

    def y_up(k):
        return remote(
            vb.at[k, :, pl.ds(ey - PACK, PACK)], halo_y.at[k, 0], sy.at[k, 0], ry.at[k, 0],
            (s, jnp.minimum(p + 1, patches - 1)),
        )

    def y_down(k):
        return remote(
            vb.at[k, :, pl.ds(0, PACK)], halo_y.at[k, 1], sy.at[k, 1], ry.at[k, 1], (s, jnp.maximum(p - 1, 0))
        )

    def d_up():
        return remote(
            disp_ref.at[:, pl.ds(rows - EDGE, EDGE)], halo_d.at[0], sd.at[0], rd.at[0],
            (s, jnp.minimum(p + 1, patches - 1)),
        )

    def d_down():
        return remote(disp_ref.at[:, pl.ds(0, EDGE)], halo_d.at[1], sd.at[1], rd.at[1], (s, jnp.maximum(p - 1, 0)))

    has_prev_s, has_next_s = s > 0, s < slabs - 1
    has_prev_p, has_next_p = p > 0, p < patches - 1

    def point_first(j, mine):
        peer = patch_peer(j)
        src = point_ref.at[0, :, pl.ds(pl.multiple_of(peer * cap, cap), cap)]
        slot = p if mine else peer
        return remote(src, points.at[s, slot], sp1.at[j], rp1.at[slot], (s, peer))

    def point_second(j, mine):
        peer = slab_peer(j)
        slot = s if mine else peer
        return remote(points.at[s], points.at[slot], sp2.at[j], rp2.at[slot], (peer, p))

    def pull_first(j, mine):
        peer = patch_peer(j)
        slot = p if mine else peer
        return remote(pull_out.at[peer], pulls.at[s, slot], sq1.at[j], rq1.at[slot], (s, peer))

    def pull_second(j, mine):
        peer = slab_peer(j)
        slot = s if mine else peer
        return remote(pulls.at[s], pulls.at[slot], sq2.at[j], rq2.at[slot], (peer, p))

    def pick_copy(j, mine):
        peer = patch_peer(j)
        slot = p if mine else peer
        return remote(picks_out.at[peer], picks_in.at[slot], sw.at[j], rw.at[slot], (s, peer))

    def send_halos(k):
        pl.when(has_next_s)(lambda: x_up(k).start())
        pl.when(has_prev_s)(lambda: x_down(k).start())
        pl.when(has_next_p)(lambda: y_up(k).start())
        pl.when(has_prev_p)(lambda: y_down(k).start())

    scales = [column(scale_ref[i : i + 1, :]) for i in range(ex)]
    inverses = [1.0 / x for x in scales]

    def build_points(slab):
        for k in range(patches):
            row, col = split_point(points[slab, k], cols)
            span = pl.ds(k * cap, cap)
            onehot_row[slab, :, span] = jnp.where(
                lax.broadcasted_iota(jnp.int32, (rows, cap), 0) == row, 1.0, 0.0
            ).astype(BF16)
            onehot_col[slab, :, span] = jnp.where(
                lax.broadcasted_iota(jnp.int32, (cols, cap), 0) == col, 1.0, 0.0
            ).astype(BF16)

    def lives(k):
        lane = lax.broadcasted_iota(jnp.int32, (1, cap), 1)
        return lane < count_ref[0, :, k : k + 1]

    def shell():
        pl.when(has_prev_p)(lambda: d_up().wait_recv())
        pl.when(has_next_p)(lambda: d_down().wait_recv())
        total = rows + 2 * EDGE
        line = lax.broadcasted_iota(jnp.int32, (total, cols), 0)
        first = jnp.where(has_prev_p, 0, EDGE)
        last = jnp.where(has_next_p, total, EDGE + rows)
        valid = (line >= first) & (line < last)
        for c in range(comps):
            field = jnp.concatenate([halo_d[0, c], disp_ref[c], halo_d[1, c]], axis=0)
            field = jnp.where(valid, field, 0.0)
            bend = jnp.where(valid, laplace(field), 0.0)
            full = (laplace(bend) + 4.0 * bend)[EDGE : EDGE + rows]
            kd_buf[c] = stiff_ref[...] * full

    v = state_ref[...]
    for k in range(SWEEPS):
        rounded = v.astype(BF16)
        vb[k] = rounded
        if k > 0:
            send_halos(k)
        own = dot(rounded.reshape(ex * ey, dof), matrix_ref[...]).reshape(ex, ey, dof)
        base = [rhs_ref[i] - scales[i] * own[i] for i in range(ex)]
        if k == 0:
            for owner in range(patches):
                elem = elem_ref[0, :, owner * cap : (owner + 1) * cap]
                hit = (lax.broadcasted_iota(jnp.int32, (ex * ey, cap), 0) == elem) & lives(owner)
                onehot_elem[owner] = jnp.where(hit, 1.0, 0.0).astype(BF16)
            for owner in range(patches):

                @pl.when(p == owner)
                def _():
                    points[s, owner] = point_ref[0, :, owner * cap : (owner + 1) * cap]

            pl.semaphore_wait(barrier, slabs - 1 + patches - 1)
            send_halos(0)
            for j in range(1, patches):
                point_first(j, True).start()
            pl.when(has_next_p)(lambda: d_up().start())
            pl.when(has_prev_p)(lambda: d_down().start())
        if k == 1:
            for j in range(1, patches):
                point_first(j, False).wait_recv()
            for j in range(1, slabs):
                point_second(j, True).start()
            build_points(s)
            shell()
        if k == 2:

            def arrive(j, carry):
                point_second(j, False).wait_recv()
                build_points(slab_peer(j))
                return carry

            lax.fori_loop(1, slabs, arrive, 0)

        wide = rounded.astype(F32)
        pl.when(has_prev_p)(lambda: y_up(k).wait_recv())
        pl.when(has_next_p)(lambda: y_down(k).wait_recv())
        line = lax.broadcasted_iota(jnp.int32, (ey, dof), 0)
        along_y = []
        for i in range(ex):
            before = halo_y[k, 0, i].astype(F32)[PACK - 1 : PACK]
            after = halo_y[k, 1, i].astype(F32)[0:1]
            before = jnp.where(has_prev_p, before, 0.0)
            after = jnp.where(has_next_p, after, 0.0)
            prev = jnp.where(line == 0, jnp.broadcast_to(before, (ey, dof)), pltpu.roll(wide[i], 1, 0))
            following = jnp.where(line == ey - 1, jnp.broadcast_to(after, (ey, dof)), pltpu.roll(wide[i], ey - 1, 0))
            along_y.append((prev + following).astype(BF16))
        side_y = dot(jnp.concatenate(along_y, axis=0), cy_ref[...])
        pl.when(has_prev_s)(lambda: x_up(k).wait_recv())
        pl.when(has_next_s)(lambda: x_down(k).wait_recv())
        low = jnp.where(has_prev_s, halo_x[k, 0].astype(F32), 0.0)
        high = jnp.where(has_next_s, halo_x[k, 1].astype(F32), 0.0)
        along_x = []
        for i in range(ex):
            below = low if i == 0 else wide[i - 1]
            above = high if i == ex - 1 else wide[i + 1]
            along_x.append((below + above).astype(BF16))
        side_x = dot(jnp.concatenate(along_x, axis=0), cx_ref[...])
        side = (side_x + side_y).reshape(ex, ey, dof)
        residue = jnp.concatenate([(base[i] + side[i]).astype(BF16) for i in range(ex)], axis=0)
        update = dot(residue, inverse_ref[...]).reshape(ex, ey, dof)
        v = jnp.stack([v[i] + update[i] * inverses[i] for i in range(ex)], axis=0)

    final = v.astype(BF16).reshape(ex * ey, dof)
    traction = dot_nt(traction_ref[...], final).astype(BF16)
    for owner in range(patches):
        pull_out[owner] = dot(traction, onehot_elem[owner]).astype(BF16)
    for j in range(1, patches):
        pull_first(j, True).start()
    pulls[s, p] = pull_out[p]
    fluid_ref[...] = v
    for j in range(1, patches):
        pull_first(j, False).wait_recv()
    for j in range(1, slabs):
        pull_second(j, True).start()

    def scatter(slab, acc):
        for k in range(patches):
            span = pl.ds(k * cap, cap)
            hot = onehot_row[slab, :, span]
            value = pulls[slab, k]
            scaled = jnp.concatenate([hot * value[c : c + 1] for c in range(comps)], axis=0)
            acc = acc + dot_nt(scaled, onehot_col[slab, :, span])
        return acc

    acc = scatter(s, jnp.zeros((comps * rows, cols), F32))

    def gathered(j, acc):
        pull_second(j, False).wait_recv()
        return scatter(slab_peer(j), acc)

    acc = lax.fori_loop(1, slabs, gathered, acc)
    loads = acc.reshape(comps, rows, cols)
    gain = 1.0 / (36.0 * stiff_ref[...])
    fresh = [disp_ref[c] + (loads[c] - kd_buf[c]) * gain for c in range(comps)]
    narrow = jnp.concatenate([x.astype(BF16) for x in fresh], axis=0)
    for k in range(patches):
        span = pl.ds(k * cap, cap)
        spread = dot(narrow, onehot_col[s, :, span]).reshape(comps, rows, cap)
        hot = onehot_row[s, :, span].astype(F32)
        for c in range(comps):
            picks_out[k, c : c + 1] = jnp.sum(spread[c] * hot, axis=0, keepdims=True)
    for j in range(1, patches):
        pick_copy(j, True).start()
    picks_in[p] = picks_out[p]
    for c in range(comps):
        net_ref[c] = fresh[c]
    for j in range(1, patches):
        pick_copy(j, False).wait_recv()
    for k in range(patches):
        live = lives(k)
        for c in range(comps):
            wall_ref[c, 0, :, k * cap : (k + 1) * cap] = jnp.where(live, picks_in[k, c : c + 1], 0.0)

    for k in range(SWEEPS):
        pl.when(has_next_s)(lambda: x_up(k).wait_send())
        pl.when(has_prev_s)(lambda: x_down(k).wait_send())
        pl.when(has_next_p)(lambda: y_up(k).wait_send())
        pl.when(has_prev_p)(lambda: y_down(k).wait_send())
    pl.when(has_next_p)(lambda: d_up().wait_send())
    pl.when(has_prev_p)(lambda: d_down().wait_send())
    for j in range(1, patches):
        point_first(j, True).wait_send()
        pull_first(j, True).wait_send()
        pick_copy(j, True).wait_send()
    for j in range(1, slabs):
        point_second(j, True).wait_send()
        pull_second(j, True).wait_send()


def shards(slabs, patches, *args):
    state, disp, elem = args[0], args[11], args[8]
    ex, ey, dof = state.shape
    comps, rows, cols = disp.shape
    cap = elem.shape[2] // patches
    sem = pltpu.SemaphoreType.DMA
    vmem = pl.BlockSpec(memory_space=pltpu.VMEM)
    return pl.pallas_call(
        functools.partial(kernel, slabs, patches),
        out_shape=(
            jax.ShapeDtypeStruct(state.shape, F32),
            jax.ShapeDtypeStruct(disp.shape, F32),
            jax.ShapeDtypeStruct((comps, 1, 1, elem.shape[2]), F32),
        ),
        in_specs=[vmem] * len(args),
        out_specs=(vmem, vmem, vmem),
        scratch_shapes=[
            pltpu.VMEM((SWEEPS, ex, ey, dof), BF16),
            pltpu.VMEM((SWEEPS, 2, ey, dof), BF16),
            pltpu.VMEM((SWEEPS, 2, ex, PACK, dof), BF16),
            pltpu.VMEM((2, comps, EDGE, cols), F32),
            pltpu.VMEM((slabs, patches, 1, cap), jnp.int32),
            pltpu.VMEM((slabs, patches, comps, cap), BF16),
            pltpu.VMEM((patches, comps, cap), BF16),
            pltpu.VMEM((patches, comps, cap), F32),
            pltpu.VMEM((patches, comps, cap), F32),
            pltpu.VMEM((patches, ex * ey, cap), BF16),
            pltpu.VMEM((slabs, rows, patches * cap), BF16),
            pltpu.VMEM((slabs, cols, patches * cap), BF16),
            pltpu.VMEM((comps, rows, cols), F32),
            sem((SWEEPS, 2)),
            sem((SWEEPS, 2)),
            sem((SWEEPS, 2)),
            sem((SWEEPS, 2)),
            sem((2,)),
            sem((2,)),
            sem((patches,)),
            sem((patches,)),
            sem((slabs,)),
            sem((slabs,)),
            sem((patches,)),
            sem((patches,)),
            sem((slabs,)),
            sem((slabs,)),
            sem((patches,)),
            sem((patches,)),
        ],
        compiler_params=pltpu.CompilerParams(collective_id=0, has_side_effects=True),
    )(*args)


def solution(mesh):
    return jax.shard_map(
        functools.partial(shards, mesh.shape["slab"], mesh.shape["patch"]),
        mesh=mesh,
        in_specs=(
            P("slab", "patch", None),
            P("slab", "patch", None),
            P("slab", "patch"),
            P(),
            P(),
            P(),
            P(),
            P(),
            P("slab", "patch", None),
            P("slab", "patch", None),
            P("slab", "patch", None),
            P(None, "patch", None),
            P("patch", None),
        ),
        out_specs=(
            P("slab", "patch", None),
            P(None, "patch", None),
            P(None, "slab", "patch", None),
        ),
        check_vma=False,
    )
```

```python
import functools

import jax
import jax.numpy as jnp
from jax import lax
from jax.experimental import pallas as pl
from jax.experimental.pallas import tpu as pltpu
from jax.sharding import PartitionSpec as P

SWEEPS = 3
PACK = 16
EDGE = 8
SPARE = 8 * 2**20
LOAD_ORDER = (0, 2, 3, 1, 8, 10, 9, 11, 12, 5, 4, 6, 7)
MESH = pl.DeviceIdType.MESH
F32 = jnp.float32
BF16 = jnp.bfloat16


def dot(a, b):
    return jnp.dot(a, b, preferred_element_type=F32)


def dot_nt(a, b):
    return lax.dot_general(a, b, (((1,), (1,)), ((), ())), preferred_element_type=F32)


def split_point(point, cols):
    if cols & (cols - 1) == 0:
        return lax.shift_right_logical(point, cols.bit_length() - 1), point & (cols - 1)
    row = lax.div(point, cols)
    return row, point - row * cols


def column(row_vector):
    n = row_vector.shape[1]
    shape = (n, n)
    eye = lax.broadcasted_iota(jnp.int32, shape, 0) == lax.broadcasted_iota(jnp.int32, shape, 1)
    return jnp.sum(jnp.where(eye, jnp.broadcast_to(row_vector, shape), 0.0), axis=1, keepdims=True)


def laplace(x):
    rows, cols = x.shape
    lane = lax.broadcasted_iota(jnp.int32, x.shape, 1)
    left = jnp.where(lane == 0, 0.0, pltpu.roll(x, 1, 1))
    right = jnp.where(lane == cols - 1, 0.0, pltpu.roll(x, cols - 1, 1))
    return 4.0 * x - (pltpu.roll(x, 1, 0) + pltpu.roll(x, rows - 1, 0) + left + right)


def kernel(slabs, patches, args, *refs):
    hbm, refs = refs[:args], refs[args:]
    (fluid_ref, net_ref, wall_ref), refs = refs[:3], refs[3:]
    staged, refs = refs[:args], refs[args:]
    (state_ref, rhs_ref, scale_ref, matrix_ref, cx_ref, cy_ref, inverse_ref, traction_ref) = staged[:8]
    (elem_ref, point_ref, count_ref, disp_ref, stiff_ref) = staged[8:]
    (vb, halo_x, halo_y, halo_d, points, pulls, pull_out, picks_out, picks_in) = refs[:9]
    (onehot_elem, onehot_row, onehot_col, rest_buf, gain_buf) = refs[9:14]
    (load_sem, sx, rx, sy, ry, sd, rd, sp1, rp1, sp2, rp2, sq1, rq1, sq2, rq2, sw, rw, near_sem) = refs[14:]

    loads_in = [pltpu.make_async_copy(hbm[n], staged[n], load_sem.at[n]) for n in range(args)]
    for n in LOAD_ORDER:
        loads_in[n].start()

    def ready(*names):
        for n in names:
            loads_in[n].wait()

    s = lax.axis_index("slab")
    p = lax.axis_index("patch")
    ex, ey, dof = state_ref.shape
    comps, rows, cols = disp_ref.shape
    cap = elem_ref.shape[2] // patches

    def slab_peer(j):
        return lax.rem(s + j, slabs)

    def patch_peer(j):
        return lax.rem(p + j, patches)

    def slab_sides(reach, semaphore):
        @pl.when(s >= reach)
        def _():
            pl.semaphore_signal(semaphore, inc=1, device_id=(s - reach, p), device_id_type=MESH)

        @pl.when(s + reach < slabs)
        def _():
            pl.semaphore_signal(semaphore, inc=1, device_id=(s + reach, p), device_id_type=MESH)

    def slab_count(reach):
        return jnp.where(s >= reach, 1, 0) + jnp.where(s + reach < slabs, 1, 0)

    reaches = []
    while 2 ** (len(reaches) + 1) < slabs - 1:
        reaches.append(2 ** (len(reaches) + 1))

    def near_signal(n):
        slab_sides(reaches[n], near_sem.at[n])

    def near_wait(n):
        pl.semaphore_wait(near_sem.at[n], slab_count(reaches[n]))

    barrier = pltpu.get_barrier_semaphore()
    for j in range(1, patches):
        pl.semaphore_signal(barrier, inc=1, device_id=(s, patch_peer(j)), device_id_type=MESH)
    slab_sides(1, barrier)
    awaited = patches - 1 + slab_count(1)

    def remote(src, dst, send, recv, target):
        return pltpu.make_async_remote_copy(
            src_ref=src, dst_ref=dst, send_sem=send, recv_sem=recv, device_id=target, device_id_type=MESH
        )

    def x_up(k):
        return remote(vb.at[k, ex - 1], halo_x.at[k, 0], sx.at[k, 0], rx.at[k, 0], (jnp.minimum(s + 1, slabs - 1), p))

    def x_down(k):
        return remote(vb.at[k, 0], halo_x.at[k, 1], sx.at[k, 1], rx.at[k, 1], (jnp.maximum(s - 1, 0), p))

    def y_up(k):
        return remote(
            vb.at[k, :, pl.ds(ey - PACK, PACK)], halo_y.at[k, 0], sy.at[k, 0], ry.at[k, 0],
            (s, jnp.minimum(p + 1, patches - 1)),
        )

    def y_down(k):
        return remote(
            vb.at[k, :, pl.ds(0, PACK)], halo_y.at[k, 1], sy.at[k, 1], ry.at[k, 1], (s, jnp.maximum(p - 1, 0))
        )

    def d_up():
        return remote(
            disp_ref.at[:, pl.ds(rows - EDGE, EDGE)], halo_d.at[0], sd.at[0], rd.at[0],
            (s, jnp.minimum(p + 1, patches - 1)),
        )

    def d_down():
        return remote(disp_ref.at[:, pl.ds(0, EDGE)], halo_d.at[1], sd.at[1], rd.at[1], (s, jnp.maximum(p - 1, 0)))

    has_prev_s, has_next_s = s > 0, s < slabs - 1
    has_prev_p, has_next_p = p > 0, p < patches - 1

    def point_first(j, mine):
        peer = patch_peer(j)
        src = point_ref.at[0, :, pl.ds(pl.multiple_of(peer * cap, cap), cap)]
        slot = p if mine else peer
        return remote(src, points.at[s, slot], sp1.at[j], rp1.at[slot], (s, peer))

    def point_second(j, mine):
        peer = slab_peer(j)
        slot = s if mine else peer
        return remote(points.at[s], points.at[slot], sp2.at[j], rp2.at[slot], (peer, p))

    def pull_first(j, mine):
        peer = patch_peer(j)
        slot = p if mine else peer
        return remote(pull_out.at[peer], pulls.at[s, slot], sq1.at[j], rq1.at[slot], (s, peer))

    def pull_second(j, mine):
        peer = slab_peer(j)
        slot = s if mine else peer
        return remote(pulls.at[s], pulls.at[slot], sq2.at[j], rq2.at[slot], (peer, p))

    def pick_copy(j, mine):
        peer = patch_peer(j)
        slot = p if mine else peer
        return remote(picks_out.at[peer], picks_in.at[slot], sw.at[j], rw.at[slot], (s, peer))

    def send_halos(k):
        pl.when(has_next_s)(lambda: x_up(k).start())
        pl.when(has_prev_s)(lambda: x_down(k).start())
        pl.when(has_next_p)(lambda: y_up(k).start())
        pl.when(has_prev_p)(lambda: y_down(k).start())

    ready(2)
    scales = [column(scale_ref[i : i + 1, :]) for i in range(ex)]
    inverses = [1.0 / x for x in scales]

    def build_points(slab):
        for k in range(patches):
            row, col = split_point(points[slab, k], cols)
            span = pl.ds(k * cap, cap)
            onehot_row[slab, :, span] = jnp.where(
                lax.broadcasted_iota(jnp.int32, (rows, cap), 0) == row, 1.0, 0.0
            ).astype(BF16)
            onehot_col[slab, :, span] = jnp.where(
                lax.broadcasted_iota(jnp.int32, (cols, cap), 0) == col, 1.0, 0.0
            ).astype(BF16)

    def lives(k):
        lane = lax.broadcasted_iota(jnp.int32, (1, cap), 1)
        return lane < count_ref[0, :, k : k + 1]

    def shell():
        pl.when(has_prev_p)(lambda: d_up().wait_recv())
        pl.when(has_next_p)(lambda: d_down().wait_recv())
        total = rows + 2 * EDGE
        line = lax.broadcasted_iota(jnp.int32, (total, cols), 0)
        first = jnp.where(has_prev_p, 0, EDGE)
        last = jnp.where(has_next_p, total, EDGE + rows)
        valid = (line >= first) & (line < last)
        gain = 1.0 / (36.0 * stiff_ref[...])
        gain_buf[...] = gain
        for c in range(comps):
            field = jnp.concatenate([halo_d[0, c], disp_ref[c], halo_d[1, c]], axis=0)
            field = jnp.where(valid, field, 0.0)
            bend = jnp.where(valid, laplace(field), 0.0)
            full = (laplace(bend) + 4.0 * bend)[EDGE : EDGE + rows]
            rest_buf[c] = disp_ref[c] - stiff_ref[...] * full * gain

    ready(0)
    v = state_ref[...]
    for k in range(SWEEPS):
        rounded = v.astype(BF16)
        vb[k] = rounded
        if k > 0:
            send_halos(k)
        if k == 0:
            ready(3, 1)
        own = dot(rounded.reshape(ex * ey, dof), matrix_ref[...]).reshape(ex, ey, dof)
        base = [rhs_ref[i] - scales[i] * own[i] for i in range(ex)]
        if k == 0:
            ready(8, 9, 10)
            for owner in range(patches):
                elem = elem_ref[0, :, owner * cap : (owner + 1) * cap]
                hit = (lax.broadcasted_iota(jnp.int32, (ex * ey, cap), 0) == elem) & lives(owner)
                onehot_elem[owner] = jnp.where(hit, 1.0, 0.0).astype(BF16)
            for owner in range(patches):

                @pl.when(p == owner)
                def _():
                    points[s, owner] = point_ref[0, :, owner * cap : (owner + 1) * cap]

            pl.semaphore_wait(barrier, awaited)
            send_halos(0)
            for j in range(1, patches):
                point_first(j, True).start()
            ready(11, 12)
            pl.when(has_next_p)(lambda: d_up().start())
            pl.when(has_prev_p)(lambda: d_down().start())
            ready(5, 4, 6, 7)
        if k == 1:
            if reaches:
                near_wait(0)
                if len(reaches) > 1:
                    near_signal(1)
            for j in range(1, patches):
                point_first(j, False).wait_recv()
            build_points(s)
        if k == 2:
            for n in range(1, len(reaches)):
                near_wait(n)
                if n + 1 < len(reaches):
                    near_signal(n + 1)
            for j in range(1, slabs):
                point_second(j, True).start()
            shell()

        wide = rounded.astype(F32)
        pl.when(has_prev_p)(lambda: y_up(k).wait_recv())
        pl.when(has_next_p)(lambda: y_down(k).wait_recv())
        line = lax.broadcasted_iota(jnp.int32, (ey, dof), 0)
        along_y = []
        for i in range(ex):
            before = halo_y[k, 0, i].astype(F32)[PACK - 1 : PACK]
            after = halo_y[k, 1, i].astype(F32)[0:1]
            before = jnp.where(has_prev_p, before, 0.0)
            after = jnp.where(has_next_p, after, 0.0)
            prev = jnp.where(line == 0, jnp.broadcast_to(before, (ey, dof)), pltpu.roll(wide[i], 1, 0))
            following = jnp.where(line == ey - 1, jnp.broadcast_to(after, (ey, dof)), pltpu.roll(wide[i], ey - 1, 0))
            along_y.append((prev + following).astype(BF16))
        side_y = dot(jnp.concatenate(along_y, axis=0), cy_ref[...])
        pl.when(has_prev_s)(lambda: x_up(k).wait_recv())
        pl.when(has_next_s)(lambda: x_down(k).wait_recv())
        if k == 0 and reaches:
            near_signal(0)
        low = jnp.where(has_prev_s, halo_x[k, 0].astype(F32), 0.0)
        high = jnp.where(has_next_s, halo_x[k, 1].astype(F32), 0.0)
        along_x = []
        for i in range(ex):
            below = low if i == 0 else wide[i - 1]
            above = high if i == ex - 1 else wide[i + 1]
            along_x.append((below + above).astype(BF16))
        side_x = dot(jnp.concatenate(along_x, axis=0), cx_ref[...])
        side = (side_x + side_y).reshape(ex, ey, dof)
        residue = jnp.concatenate([(base[i] + side[i]).astype(BF16) for i in range(ex)], axis=0)
        update = dot(residue, inverse_ref[...]).reshape(ex, ey, dof)
        v = jnp.stack([v[i] + update[i] * inverses[i] for i in range(ex)], axis=0)

    final = v.astype(BF16).reshape(ex * ey, dof)
    traction = dot_nt(traction_ref[...], final).astype(BF16)
    for owner in range(patches):
        pull_out[owner] = dot(traction, onehot_elem[owner]).astype(BF16)
    for j in range(1, patches):
        pull_first(j, True).start()
    pulls[s, p] = pull_out[p]
    fluid_ref[...] = v
    for j in range(1, patches):
        pull_first(j, False).wait_recv()
    for j in range(1, slabs):
        pull_second(j, True).start()

    def scatter(slab, acc):
        for k in range(patches):
            span = pl.ds(k * cap, cap)
            hot = onehot_row[slab, :, span]
            value = pulls[slab, k]
            scaled = jnp.concatenate([hot * value[c : c + 1] for c in range(comps)], axis=0)
            acc = acc + dot_nt(scaled, onehot_col[slab, :, span])
        return acc

    def arrive(j, carry):
        point_second(j, False).wait_recv()
        build_points(slab_peer(j))
        return carry

    lax.fori_loop(1, slabs, arrive, 0)
    acc = scatter(s, jnp.zeros((comps * rows, cols), F32))

    def gathered(j, acc):
        pull_second(j, False).wait_recv()
        return scatter(slab_peer(j), acc)

    acc = lax.fori_loop(1, slabs, gathered, acc)
    loads = acc.reshape(comps, rows, cols)
    fresh = [rest_buf[c] + loads[c] * gain_buf[...] for c in range(comps)]
    narrow = jnp.concatenate([x.astype(BF16) for x in fresh], axis=0)
    for k in range(patches):
        span = pl.ds(k * cap, cap)
        spread = dot(narrow, onehot_col[s, :, span]).reshape(comps, rows, cap)
        hot = onehot_row[s, :, span].astype(F32)
        for c in range(comps):
            picks_out[k, c : c + 1] = jnp.sum(spread[c] * hot, axis=0, keepdims=True)
    for j in range(1, patches):
        pick_copy(j, True).start()
    picks_in[p] = picks_out[p]
    for c in range(comps):
        net_ref[c] = fresh[c]
    for j in range(1, patches):
        pick_copy(j, False).wait_recv()
    for k in range(patches):
        live = lives(k)
        for c in range(comps):
            wall_ref[c, 0, :, k * cap : (k + 1) * cap] = jnp.where(live, picks_in[k, c : c + 1], 0.0)

    for k in range(SWEEPS):
        pl.when(has_next_s)(lambda: x_up(k).wait_send())
        pl.when(has_prev_s)(lambda: x_down(k).wait_send())
        pl.when(has_next_p)(lambda: y_up(k).wait_send())
        pl.when(has_prev_p)(lambda: y_down(k).wait_send())
    pl.when(has_next_p)(lambda: d_up().wait_send())
    pl.when(has_prev_p)(lambda: d_down().wait_send())
    for j in range(1, patches):
        point_first(j, True).wait_send()
        pull_first(j, True).wait_send()
        pick_copy(j, True).wait_send()
    for j in range(1, slabs):
        point_second(j, True).wait_send()
        pull_second(j, True).wait_send()


def deliver(*refs):
    copies = [pltpu.make_async_copy(refs[n], refs[n + 3], refs[6].at[n]) for n in range(3)]
    for copy in copies:
        copy.start()
    for copy in copies:
        copy.wait()


def shards(slabs, patches, *args):
    state, disp, elem = args[0], args[11], args[8]
    ex, ey, dof = state.shape
    comps, rows, cols = disp.shape
    cap = elem.shape[2] // patches
    sem = pltpu.SemaphoreType.DMA
    vmem = pl.BlockSpec(memory_space=pltpu.VMEM)
    hot_bytes = slabs * patches * cap * (rows + cols) * 2
    outs = pl.pallas_call(
        functools.partial(kernel, slabs, patches, len(args)),
        out_shape=(
            jax.ShapeDtypeStruct(state.shape, F32),
            jax.ShapeDtypeStruct(disp.shape, F32),
            jax.ShapeDtypeStruct((comps, 1, 1, elem.shape[2]), F32),
        ),
        in_specs=[pl.BlockSpec(memory_space=pltpu.HBM)] * len(args),
        out_specs=(vmem, vmem, vmem),
        scratch_shapes=[pltpu.VMEM(x.shape, x.dtype) for x in args]
        + [
            pltpu.VMEM((SWEEPS, ex, ey, dof), BF16),
            pltpu.VMEM((SWEEPS, 2, ey, dof), BF16),
            pltpu.VMEM((SWEEPS, 2, ex, PACK, dof), BF16),
            pltpu.VMEM((2, comps, EDGE, cols), F32),
            pltpu.VMEM((slabs, patches, 1, cap), jnp.int32),
            pltpu.VMEM((slabs, patches, comps, cap), BF16),
            pltpu.VMEM((patches, comps, cap), BF16),
            pltpu.VMEM((patches, comps, cap), F32),
            pltpu.VMEM((patches, comps, cap), F32),
            pltpu.VMEM((patches, ex * ey, cap), BF16),
            pltpu.VMEM((slabs, rows, patches * cap), BF16),
            pltpu.VMEM((slabs, cols, patches * cap), BF16),
            pltpu.VMEM((comps, rows, cols), F32),
            pltpu.VMEM((rows, cols), F32),
            sem((len(args),)),
            sem((SWEEPS, 2)),
            sem((SWEEPS, 2)),
            sem((SWEEPS, 2)),
            sem((SWEEPS, 2)),
            sem((2,)),
            sem((2,)),
            sem((patches,)),
            sem((patches,)),
            sem((slabs,)),
            sem((slabs,)),
            sem((patches,)),
            sem((patches,)),
            sem((slabs,)),
            sem((slabs,)),
            sem((patches,)),
            sem((patches,)),
            pltpu.SemaphoreType.REGULAR((max(slabs.bit_length(), 1),)),
        ],
        compiler_params=pltpu.CompilerParams(collective_id=0, has_side_effects=True),
    )(*args)
    return pl.pallas_call(
        deliver,
        out_shape=tuple(jax.ShapeDtypeStruct(x.shape, x.dtype) for x in outs),
        in_specs=[vmem] * 3,
        out_specs=(pl.BlockSpec(memory_space=pltpu.HBM),) * 3,
        scratch_shapes=[sem((3,))],
    )(*outs)


def solution(mesh):
    return jax.shard_map(
        functools.partial(shards, mesh.shape["slab"], mesh.shape["patch"]),
        mesh=mesh,
        in_specs=(
            P("slab", "patch", None),
            P("slab", "patch", None),
            P("slab", "patch"),
            P(),
            P(),
            P(),
            P(),
            P(),
            P("slab", "patch", None),
            P("slab", "patch", None),
            P("slab", "patch", None),
            P(None, "patch", None),
            P("patch", None),
        ),
        out_specs=(
            P("slab", "patch", None),
            P(None, "patch", None),
            P(None, "slab", "patch", None),
        ),
        check_vma=False,
    )
```
